32 devices in a mesh: dp: 8 (over y, x, core), tensor: 4 (over z).
Axes of the slice: x: 2, y: 2, z: 4, core: 2. Of those that a mesh axis runs over, the one named last changes fastest.
Arguments:
- gate_pre: bfloat16 [3072, 14336], P('dp', 'tensor'), may hold values from -6 to 6
- up_pre: bfloat16 [3072, 14336], P('dp', 'tensor'), may hold values from -6 to 6
- out_grad: bfloat16 [3072, 4096], P('dp'), may hold values from -6 to 6
- old_weight: float32 [14336, 4096], P(('dp', 'tensor')), may hold values from -0.046875 to 0.046875
- old_first: float32 [14336, 4096], P(('dp', 'tensor')), may hold values from -8 to 8
- old_second: float32 [14336, 4096], P(('dp', 'tensor')), may hold values from 1 to 1000
Outputs:
- new_weight: float32 [14336, 4096], P('tensor', 'dp')
- new_first: float32 [14336, 4096], P('tensor', 'dp')
- new_second: float32 [14336, 4096], P('tensor', 'dp')
- grad_gate: bfloat16 [3072, 14336], P('dp', 'tensor')
- grad_up: bfloat16 [3072, 14336], P('dp', 'tensor')
The draws below stay inside these ranges and needn't reach their ends.
All inputs are finite; a program needn't handle non-finite values.
Results may differ from the reference program's by a relative error of at most 0.0051.
Values may be sent and summed in bfloat16 or wider, within the bound.
No kernel may reach another device: no remote copies, remote signals or barrier semaphores. Data moves between devices by JAX's collectives and lax.ppermute only.
A program may use at most 256 MiB of HBM per device.

```python
import math
import jax
import jax.numpy as jnp
from jax import lax

D = 4096
FF = 14336
TOK_DEV = 384
TOKENS = 3072
N_DP = 8


def raised(values, own_key, source, target, blocks, factor):
    def block_of(dim):
        return (jnp.arange(values.shape[dim]) // (values.shape[dim] // blocks)).reshape((-1,) + (1,) * (values.ndim - 1 - dim))

    first = jax.random.permutation(own_key, blocks)[block_of(target)]
    far = (block_of(target) + blocks // 2) % blocks
    return jnp.where((block_of(source) == first) | (block_of(source) == far), factor * values, values)


def steps_of(stream_key, extent, shards, low, high):
    def one(position, parts):
        steps = jax.random.uniform(jax.random.fold_in(jax.random.fold_in(stream_key, 6), position), (parts,), jnp.float32, low / len(shards), high / len(shards))
        return jnp.repeat(jnp.exp(steps), extent[position] // parts).reshape((-1,) + (1,) * (len(extent) - position - 1))

    loudness = one(*shards[0])
    for cut in shards[1:]:
        loudness = loudness * one(*cut)
    return loudness


def noise(key, shape, spread, bound, shards=(), kind=jnp.bfloat16):
    entries = spread * jax.random.normal(key, shape, jnp.float32)
    if shards:
        entries = entries * steps_of(key, shape, shards, -0.22, 0.18)
    return jnp.clip(entries, -bound, bound).astype(kind)


def bell_draw_with(key, shape, width, most, shards, heavy, held_as=jnp.bfloat16):
    drawn = width * jax.random.normal(key, shape, jnp.float32)
    if shards:
        drawn = drawn * steps_of(key, shape, shards, -0.22, 0.18)
    return jnp.clip(raised(drawn, jax.random.fold_in(key, 3), *heavy), -most, most).astype(held_as)


def setup_inputs(seed: int = 0) -> dict:
    streams_of = jax.random.split(jax.random.key(seed), 7)
    return {
        "gate_pre": noise(streams_of[0], (TOKENS, FF), 1.0, 6.0, ((0, 8), (1, 4))),
        "up_pre": noise(streams_of[1], (TOKENS, FF), 1.0, 6.0, ((0, 8), (1, 4))),
        "out_grad": bell_draw_with(streams_of[2], (TOKENS, D), 1.0, 6.0, ((0, 8),), (0, 1, 8, 2.0)),
        "old_weight": noise(streams_of[3], (FF, D), FF ** -0.5, 0.046875, ((0, 32),), jnp.float32),
        "old_first": noise(streams_of[4], (FF, D), 2.0, 8.0, ((0, 32),), jnp.float32),
        "old_second": jnp.clip(jnp.exp(math.log(1000.0) - 6.9077553 * jax.random.uniform(streams_of[5], (FF, D), jnp.float32) ** steps_of(streams_of[5], (FF, D), ((0, 32),), -0.2, 0.2)), 1.0, 1000.0),
    }


beta_one = 0.9
beta_two = 0.95
learn_rate = 0.0003
decay_rate = 0.1
epsilon = 1e-08
step_count = 1001

def adamw(weight, first, second, grad):
    first_new = beta_one * first + (1.0 - beta_one) * grad
    second_new = beta_two * second + (1.0 - beta_two) * grad * grad
    first_hat = first_new / (1.0 - beta_one ** step_count)
    second_hat = second_new / (1.0 - beta_two ** step_count)
    weight_new = weight - learn_rate * (first_hat / (jnp.sqrt(second_hat) + epsilon) + decay_rate * weight)
    return (weight_new, first_new, second_new)

def reference(gate_pre, up_pre, out_grad, old_weight, old_first, old_second):
    gate_f = gate_pre.astype(jnp.float32)
    up_f = up_pre.astype(jnp.float32)
    sig = jax.nn.sigmoid(gate_f)
    hidden = (gate_f * sig * up_f).astype(jnp.bfloat16)
    weight_half = old_weight.astype(jnp.bfloat16)
    hidden_grad = jnp.dot(out_grad, weight_half.T, preferred_element_type=jnp.float32)
    grad_gate = (hidden_grad * up_f * sig * (1.0 + gate_f * (1.0 - sig))).astype(jnp.bfloat16)
    grad_up = (hidden_grad * gate_f * sig).astype(jnp.bfloat16)
    hidden_parts = hidden.reshape(N_DP, TOK_DEV, FF)
    grad_parts = out_grad.reshape(N_DP, TOK_DEV, D)

    def add_block(running, pair):
        partial_grad = jnp.dot(pair[0].T, pair[1], preferred_element_type=jnp.float32)
        rounded = lax.optimization_barrier(partial_grad.astype(jnp.bfloat16)).astype(jnp.float32)
        return (running + rounded, None)
    weight_grad, unused = lax.scan(add_block, jnp.zeros((FF, D), jnp.float32), (hidden_parts, grad_parts))
    new_weight, new_first, new_second = adamw(old_weight, old_first, old_second, weight_grad)
    return (new_weight, new_first, new_second, grad_gate, grad_up)
```

```python
import jax
import jax.numpy as jnp
from jax import lax
from jax.sharding import PartitionSpec as P

beta_one = 0.9
beta_two = 0.95
learn_rate = 0.0003
decay_rate = 0.1
epsilon = 1e-08
step_count = 1001
weight_chunks = 4


def adamw(weight, first, second, grad):
    first_new = beta_one * first + (1.0 - beta_one) * grad
    second_new = beta_two * second + (1.0 - beta_two) * grad * grad
    first_hat = first_new / (1.0 - beta_one**step_count)
    second_hat = second_new / (1.0 - beta_two**step_count)
    weight_new = weight - learn_rate * (
        first_hat / (jnp.sqrt(second_hat) + epsilon) + decay_rate * weight
    )
    return (weight_new, first_new, second_new)


def body(gate_pre, up_pre, out_grad, old_weight, old_first, old_second):
    dp_count = lax.axis_size("dp")
    planes = lax.axis_size("tensor")
    chips = dp_count // 2
    dp_index = lax.axis_index("dp")
    chip, core = dp_index // 2, dp_index % 2
    plane = lax.axis_index("tensor")
    block_rows, width = old_weight.shape
    cols = width // dp_count
    tokens = out_grad.shape[0]

    def to_chip(x, step):
        return lax.ppermute(x, "dp", [(d, d ^ (2 * step)) for d in range(dp_count)])

    def to_plane(x, step):
        return lax.ppermute(x, "tensor", [(t, t ^ step) for t in range(planes)])

    def to_partner(x):
        return lax.ppermute(x, "dp", [(d, d ^ 1) for d in range(dp_count)])

    def pick(items, index):
        chosen = items[0]
        for i in range(1, len(items)):
            chosen = jnp.where(index == i, items[i], chosen)
        return chosen

    def gather_chips(x):
        if chips != 4:
            return [x] + [to_chip(x, s) for s in range(1, chips)]
        half = x.shape[0] // 2
        near_x = to_chip(x, 1)
        near_y = to_chip(x, 2)
        far_low = to_chip(near_y[:half], 1)
        far_high = to_chip(near_x[half:], 2)
        return [x, near_x, near_y, jnp.concatenate([far_low, far_high], 0)]

    def exchange(parts, name):
        n = len(parts)
        with jax.named_scope(name + "_chip"):
            cut = [
                jnp.stack(
                    [
                        lax.dynamic_slice_in_dim(p, (chip ^ s) * 2 * cols, 2 * cols, 1)
                        for p in parts
                    ]
                ).astype(jnp.bfloat16)
                for s in range(chips)
            ]
            held = [cut[0]] + [to_chip(cut[s], s) for s in range(1, chips)]
        with jax.named_scope(name + "_plane"):
            sent = [pick(held, plane ^ s ^ chip) for s in range(planes)]
            got = [sent[0]] + [to_plane(sent[s], s) for s in range(1, planes)]
        with jax.named_scope(name + "_core"):
            mine = [lax.dynamic_slice_in_dim(g, core * cols, cols, 2) for g in got]
            other = jnp.stack(
                [lax.dynamic_slice_in_dim(g, (1 - core) * cols, cols, 2) for g in got]
            )
            theirs = to_partner(other)
            tile = jnp.zeros((n, dp_count * block_rows, cols), jnp.bfloat16)
            for s in range(planes):
                row = (core * planes + (plane ^ s)) * block_rows
                tile = lax.dynamic_update_slice(tile, mine[s], (0, row, 0))
                row = ((1 - core) * planes + (plane ^ s)) * block_rows
                tile = lax.dynamic_update_slice(tile, theirs[s], (0, row, 0))
        return tile

    weight_tile = exchange([old_weight], "w")[0]
    moments = exchange([old_first, old_second], "mv")

    gate_f = gate_pre.astype(jnp.float32)
    up_f = up_pre.astype(jnp.float32)
    sig = jax.nn.sigmoid(gate_f)
    hidden = (gate_f * sig * up_f).astype(jnp.bfloat16)

    with jax.named_scope("og"):
        mine = [
            lax.dynamic_slice_in_dim(out_grad, (2 * (chip ^ s) + core) * cols, cols, 1)
            for s in range(chips)
        ]
        other = [
            lax.dynamic_slice_in_dim(out_grad, (2 * (chip ^ s) + 1 - core) * cols, cols, 1)
            for s in range(chips)
        ]
        pairs = [jnp.concatenate([a, b], 1) for a, b in zip(mine, other)]
        columns = [pairs[0]] + [to_chip(pairs[s], s) for s in range(1, chips)]
        partner_grad = to_partner(jnp.concatenate(other, 1))
        chip_grad = jnp.concatenate([jnp.concatenate(mine, 1), partner_grad], 0)

    with jax.named_scope("wg"):
        hidden_all = jnp.concatenate(gather_chips(hidden), 0)
        columns_all = jnp.concatenate(columns, 0)
        partial_grad = lax.dot_general(
            hidden_all,
            columns_all,
            (((0,), (0,)), ((), ())),
            preferred_element_type=jnp.float32,
        )
        weight_grad = partial_grad[:, :cols] + to_partner(partial_grad[:, cols:])

    new_weight, new_first, new_second = adamw(
        weight_tile.astype(jnp.float32),
        moments[0].astype(jnp.float32),
        moments[1].astype(jnp.float32),
        weight_grad,
    )

    grads = []
    step = weight_tile.shape[0] // weight_chunks
    for i in range(weight_chunks):
        with jax.named_scope(f"hg{i}"):
            blocks = gather_chips(weight_tile[i * step : (i + 1) * step])
            total = None
            for s in range(chips):
                term = lax.dot_general(
                    chip_grad[:, s * cols : (s + 1) * cols],
                    blocks[s],
                    (((1,), (1,)), ((), ())),
                    preferred_element_type=jnp.float32,
                )
                total = term if total is None else total + term
            hidden_grad = total[:tokens] + to_partner(total[tokens:])
            at = slice(i * step, (i + 1) * step)
            g, u, s = gate_f[:, at], up_f[:, at], sig[:, at]
            grads.append(
                (
                    (hidden_grad * u * s * (1.0 + g * (1.0 - s))).astype(jnp.bfloat16),
                    (hidden_grad * g * s).astype(jnp.bfloat16),
                )
            )
    grad_gate = jnp.concatenate([a for a, b in grads], 1)
    grad_up = jnp.concatenate([b for a, b in grads], 1)
    return (new_weight, new_first, new_second, grad_gate, grad_up)


def solution(mesh):
    placed = (
        P("dp", "tensor"),
        P("dp", "tensor"),
        P("dp", None),
        P(("dp", "tensor"), None),
        P(("dp", "tensor"), None),
        P(("dp", "tensor"), None),
    )
    return jax.shard_map(
        body,
        mesh=mesh,
        in_specs=placed,
        out_specs=(
            P("tensor", "dp"),
            P("tensor", "dp"),
            P("tensor", "dp"),
            P("dp", "tensor"),
            P("dp", "tensor"),
        ),
        check_vma=False,
    )
```

```python
import functools

import jax
import jax.numpy as jnp
from jax import lax
from jax.experimental import pallas as pl
from jax.experimental.pallas import tpu as pltpu
from jax.sharding import PartitionSpec as P


beta_one = 0.9
beta_two = 0.95
learn_rate = 0.0003
decay_rate = 0.1
epsilon = 1e-08
step_count = 1001


def adamw(weight, first, second, grad):
    first_new = beta_one * first + (1.0 - beta_one) * grad
    second_new = beta_two * second + (1.0 - beta_two) * grad * grad
    first_hat = first_new * (1.0 / (1.0 - beta_one**step_count))
    second_hat = second_new * (1.0 / (1.0 - beta_two**step_count))
    weight_new = weight - learn_rate * (
        first_hat / (second_hat * lax.rsqrt(second_hat) + epsilon) + decay_rate * weight
    )
    return (weight_new, first_new, second_new)


def rows_of(tokens, width, block):
    return pl.BlockSpec((tokens, width), lambda i: (block, 0))


def hidden_gradient(grads, weights, step):
    chips = len(weights)
    flat = [pair for group in grads for pair in group]
    rows, width = weights[0].shape
    tokens = flat[0][0].shape[0] // flat[0][2]

    def kernel(*refs):
        left, right, outs = refs[: 4 * chips], refs[4 * chips : 5 * chips], refs[5 * chips :]
        for n in range(4):
            total = None
            for at in range(chips):
                term = lax.dot_general(
                    left[n * chips + at][...],
                    right[at][...],
                    (((1,), (1,)), ((), ())),
                    preferred_element_type=jnp.float32,
                )
                total = term if total is None else total + term
            if n < 2:
                outs[n][...] = total
            else:
                at = (n - 2) * tokens
                outs[2][at : at + tokens] = total.astype(jnp.bfloat16)

    return pl.pallas_call(
        kernel,
        grid=(rows // step,),
        in_specs=[rows_of(tokens, width, block) for x, block, n in flat]
        + [pl.BlockSpec((step, width), lambda i: (i, 0))] * chips,
        out_specs=[pl.BlockSpec((tokens, step), lambda i: (0, i))] * 2
        + [pl.BlockSpec((2 * tokens, step), lambda i: (0, i))],
        out_shape=[jax.ShapeDtypeStruct((tokens, rows), jnp.float32)] * 2
        + [jax.ShapeDtypeStruct((2 * tokens, rows), jnp.bfloat16)],
        cost_estimate=pl.CostEstimate(
            flops=8 * chips * tokens * rows * width,
            bytes_accessed=8 * chips * tokens * width + 12 * tokens * rows,
            transcendentals=0,
        ),
        name="hidden_gradient",
    )(*[x for x, block, n in flat], *weights)


def weight_gradient(hidden, grads, step):
    chips = len(grads[0])
    flat = [pair for group in grads for pair in group]
    tokens = hidden[0].shape[0] // 2
    rows = hidden[0].shape[1]
    width = flat[0][0].shape[1]

    def kernel(*refs):
        held, right, outs = refs[:2], refs[2 : 2 + 4 * chips], refs[2 + 4 * chips :]
        for at in range(chips):
            total = None
            for n in range(4):
                low = n % 2 * tokens
                term = lax.dot_general(
                    held[n // 2][low : low + tokens],
                    right[n * chips + at][...],
                    (((0,), (0,)), ((), ())),
                    preferred_element_type=jnp.float32,
                )
                total = term if total is None else total + term
            outs[at][...] = total.astype(outs[at].dtype)

    return pl.pallas_call(
        kernel,
        grid=(rows // step,),
        in_specs=[pl.BlockSpec((2 * tokens, step), lambda i: (0, i))] * 2
        + [rows_of(tokens, width, block) for x, block, n in flat],
        out_specs=[pl.BlockSpec((step, width), lambda i: (i, 0))] * chips,
        out_shape=[
            jax.ShapeDtypeStruct((rows, width), jnp.bfloat16 if at else jnp.float32)
            for at in range(chips)
        ],
        cost_estimate=pl.CostEstimate(
            flops=8 * chips * tokens * rows * width,
            bytes_accessed=8 * chips * tokens * width + 8 * tokens * rows + 6 * rows * width,
            transcendentals=0,
        ),
        name="weight_gradient",
    )(*hidden, *[x for x, block, n in flat])


def update_half(place, side, weights, firsts, seconds, grad, so_far):
    block_rows = weights[0].shape[1]
    rows_all, cols = grad.shape
    planes = rows_all // block_rows
    cuts = 2 if block_rows % 32 == 0 else 1
    rows = block_rows // cuts
    arrays = len(weights)

    def kernel(place_ref, grad_ref, *refs):
        outs = refs[-3:]
        for n in range(arrays):

            @pl.when((pl.program_id(0) == n) | (arrays == 1))
            def _(held=refs[n : 3 * arrays : arrays]):
                new = adamw(*[ref[0].astype(jnp.float32) for ref in held], grad_ref[...])
                for out, value in zip(outs, new):
                    out[...] = value

    def row(s, i, place_ref):
        return (s ^ place_ref[1]) * cuts + i

    def grad_index(s, i, place_ref):
        return (row(s, i, place_ref), 0)

    def out_index(s, i, place_ref):
        return ((side ^ place_ref[0]) * planes * cuts + row(s, i, place_ref), 0)

    def held_index(n, s, i, place_ref):
        if arrays == 1:
            return (s, i, 0)
        return (0, jnp.clip((s - n) * cuts + i, 0, cuts - 1), place_ref[0])

    shape = jax.ShapeDtypeStruct((2 * rows_all, cols), jnp.float32)
    return pl.pallas_call(
        kernel,
        grid_spec=pltpu.PrefetchScalarGridSpec(
            num_scalar_prefetch=1,
            grid=(planes, cuts),
            in_specs=[pl.BlockSpec((rows, cols), grad_index)]
            + [
                pl.BlockSpec((1, rows, cols), functools.partial(held_index, at))
                for _ in range(3)
                for at in range(arrays)
            ]
            + [pl.BlockSpec(memory_space=pl.ANY)] * len(so_far),
            out_specs=[pl.BlockSpec((rows, cols), out_index)] * 3,
        ),
        out_shape=[shape] * 3,
        input_output_aliases={2 + 3 * arrays + n: n for n in range(len(so_far))},
        cost_estimate=pl.CostEstimate(
            flops=20 * rows_all * cols,
            bytes_accessed=22 * rows_all * cols,
            transcendentals=2 * rows_all * cols,
        ),
        name="update_half",
    )(place, grad, *weights, *firsts, *seconds, *so_far)


def body(gate_pre, up_pre, out_grad, old_weight, old_first, old_second):
    dp_count = lax.axis_size("dp")
    planes = lax.axis_size("tensor")
    chips = dp_count // 2
    dp_index = lax.axis_index("dp")
    chip, core = dp_index // 2, dp_index % 2
    plane = lax.axis_index("tensor")
    place = jnp.stack([core, plane]).astype(jnp.int32)
    block_rows, width = old_weight.shape
    cols = width // dp_count
    tokens, hidden_cols = gate_pre.shape
    half = hidden_cols // 2

    def to_chip(x, step):
        return lax.ppermute(x, "dp", [(d, d ^ (2 * step)) for d in range(dp_count)])

    def to_plane(x, step):
        return lax.ppermute(x, "tensor", [(t, t ^ step) for t in range(planes)])

    def to_partner(x):
        return lax.ppermute(x, "dp", [(d, d ^ 1) for d in range(dp_count)])

    def pick(items, index):
        chosen = items[0]
        for i in range(1, len(items)):
            chosen = jnp.where(index == i, items[i], chosen)
        return chosen

    def chip_columns(x, step):
        return lax.dynamic_slice_in_dim(x, (chip ^ step) * 2 * cols, 2 * cols, 1)

    def exchange(x):
        cut = [chip_columns(x, s).astype(jnp.bfloat16)[None] for s in range(chips)]
        held = [cut[0]] + [to_chip(cut[s], s) for s in range(1, chips)]
        sent = [pick(held, plane ^ s ^ chip) for s in range(planes)]
        return [sent[0]] + [to_plane(sent[s], s) for s in range(1, planes)]

    weight_got = exchange(old_weight)
    first_got = exchange(old_first)
    second_got = exchange(old_second)

    bits = (1, 2)
    groups = [[s for s in range(chips) if not s & bit] for bit in bits]
    step = next(n for n in (256, 128, 64) if half % n == 0 and half > n)
    blocks = half // step
    sizes = [(blocks - blocks // 2) * step, blocks // 2 * step]
    lows = [0, sizes[0]]

    pieces = [chip_columns(out_grad, s) for s in range(chips)]
    near = [
        to_chip(jnp.concatenate([pieces[s ^ bit] for s in group], 0), bit)
        for bit, group in zip(bits, groups)
    ]
    own_grad = jnp.concatenate(pieces, 0)
    own_part = to_partner(own_grad)
    near_part = [to_partner(x) for x in near]
    grads = [
        [[(x, s, chips) for s in group] for x in (own_grad, own_part)]
        + [[(x, n, len(group)) for n in range(len(group))] for x in (near[p], near_part[p])]
        for p, group in enumerate(groups)
    ]

    gate_f = gate_pre.astype(jnp.float32)
    up_f = up_pre.astype(jnp.float32)
    hidden = (gate_f * jax.nn.sigmoid(gate_f) * up_f).astype(jnp.bfloat16)
    hidden_own = lax.dynamic_slice_in_dim(hidden, core * half, half, 1)
    hidden_other = lax.dynamic_slice_in_dim(hidden, (1 - core) * half, half, 1)
    hidden_part = to_partner(hidden_other)
    hidden_held = []
    for p, bit in enumerate(bits):
        at = slice(lows[p], lows[p] + sizes[p])
        own = jnp.concatenate([hidden_own[:, at], hidden_part[:, at]], 0)
        hidden_held.append([own, to_chip(own, bit)])

    weight_grads = []
    for p, group in enumerate(groups):
        terms = weight_gradient(hidden_held[p], grads[p], step)
        came = [to_chip(terms[n], s) for n, s in enumerate(group) if n]
        weight_grads.append([terms[0]] + came)

    weight_rows = jnp.zeros((planes * block_rows, 2 * cols), jnp.bfloat16)
    for s in range(planes):
        weight_rows = lax.dynamic_update_slice(
            weight_rows, weight_got[s][0], ((plane ^ s) * block_rows, 0)
        )
    own_sum, partner_sum = [], []
    for p, (bit, group) in enumerate(zip(bits, groups)):
        own = weight_rows[lows[p] : lows[p] + sizes[p]]
        held = [own] + [to_chip(own, s) for s in group[1:]]
        kept, kept_part, sent = hidden_gradient(grads[p], held, step)
        came = to_chip(sent, bit)
        own_sum.append(kept + came[:tokens].astype(jnp.float32))
        total = kept_part + came[tokens:].astype(jnp.float32)
        partner_sum.append(to_partner(total))

    def columns_of(x, side):
        return lax.dynamic_slice_in_dim(x, side * cols, cols, x.ndim - 1)

    def other_columns(held):
        return jnp.concatenate([columns_of(x, 1 - core) for x in held], 0)

    weight_other = other_columns(weight_got)
    first_other = other_columns(first_got)
    second_other = other_columns(second_got)
    sums = [
        [sum(columns_of(x, side).astype(jnp.float32) for x in terms) for terms in weight_grads]
        for side in (core, 1 - core)
    ]
    grad_own, grad_other = (jnp.concatenate(x, 0) for x in sums)
    weight_came = to_partner(weight_other)
    first_came = to_partner(first_other)
    grad_came = to_partner(grad_other)
    second_came = to_partner(second_other)
    updated = update_half(place, 0, weight_got, first_got, second_got, grad_own, ())
    updated = update_half(place, 1, [weight_came], [first_came], [second_came], grad_came, updated)

    gate_late, up_late = lax.optimization_barrier((gate_pre, up_pre))
    own, other = jnp.concatenate(own_sum, 1), jnp.concatenate(partner_sum, 1)
    hidden_grad = jnp.where(
        core == 0, jnp.concatenate([own, other], 1), jnp.concatenate([other, own], 1)
    )
    gate_f = gate_late.astype(jnp.float32)
    up_f = up_late.astype(jnp.float32)
    sig = jax.nn.sigmoid(gate_f)
    grad_gate = (hidden_grad * up_f * sig * (1.0 + gate_f * (1.0 - sig))).astype(jnp.bfloat16)
    grad_up = (hidden_grad * gate_f * sig).astype(jnp.bfloat16)
    return (*updated, grad_gate, grad_up)


def solution(mesh):
    placed = (
        P("dp", "tensor"),
        P("dp", "tensor"),
        P("dp", None),
        P(("dp", "tensor"), None),
        P(("dp", "tensor"), None),
        P(("dp", "tensor"), None),
    )

    return jax.shard_map(
        body,
        mesh=mesh,
        in_specs=placed,
        out_specs=(
            P("tensor", "dp"),
            P("tensor", "dp"),
            P("tensor", "dp"),
            P("dp", "tensor"),
            P("dp", "tensor"),
        ),
        check_vma=False,
    )
```
